256 devices in a mesh: dp: 16 (over y, x), expert: 16 (over z, core).
Axes of the slice: x: 4, y: 4, z: 8, core: 2. Of those that a mesh axis runs over, the one named last changes fastest.
Arguments:
- tokens: float32 [2048, 2048], P('expert'), may hold values from -6 to 6
- expert_ids: int32 [2048, 8], P('expert'), may hold values from 0 to 127, all different within a row; in each aligned block of 128 rows (0 to 127, 128 to 255, ...) at most 10 rows name the same one
- gate_values: float32 [2048, 8], P('expert'), may hold values from 0.05 to 1
- valid_mask: int32 [2048], P('expert'), may hold values from 0 to 1, as said below
- gate_weight: bfloat16 [128, 1536, 2048], P('expert', 'dp'), may hold values from -0.125 to 0.125
- up_weight: bfloat16 [128, 1536, 2048], P('expert', 'dp'), may hold values from -0.125 to 0.125
- down_weight: bfloat16 [128, 1536, 2048], P('expert', 'dp'), may hold values from -0.15625 to 0.15625
Outputs:
- blended: float32 [2048, 2048], P('expert')
- loss: float32 [], replicated
The draws below stay inside these ranges and needn't reach their ends.
Inputs may be any that keep to these rules, and one draw needn't show every extreme that they name: `expert_ids`: each row names 8 different experts; in the 128 rows of one block no expert is named more than 10 times. `valid_mask`: each block of 128 tokens holds at least one valid token.
All inputs are finite; a program needn't handle non-finite values.
Results may differ from the reference program's by a relative error of at most 0.0058.
Values may be sent and summed in bfloat16 or wider, within the bound.
A program may use at most 128 MiB of HBM per device.

```python
import math
import jax
import jax.numpy as jnp
import numpy as np
from jax import lax

D = 2048
FF = 1536
TOP = 8
TOK_DEV = 128
EXPERTS = 128
CAP = 10
TOKENS = 2048


def draw_valid_mask(key, part):
    base = jax.random.fold_in(key, 17)
    key_keep = jax.random.fold_in(base, 1)
    key_pick = jax.random.fold_in(base, 2)
    kept_draw = jax.random.randint(key_keep, (TOKENS // TOK_DEV, TOK_DEV), 0, 4) > 0
    chosen = jax.random.randint(key_pick, (TOKENS // TOK_DEV,), 0, TOK_DEV)
    forced = jnp.arange(TOK_DEV, dtype=jnp.int32)[None, :] == chosen[:, None]
    return (kept_draw | forced).astype(jnp.int32).reshape(TOKENS)


def steps_of(own_key, dims, cuts, smallest, largest):
    level = 1.0
    for dim, shards_of in cuts:
        heights = jax.random.uniform(jax.random.fold_in(jax.random.fold_in(own_key, 6), dim), (shards_of,), jnp.float32, smallest / len(cuts), largest / len(cuts))
        level = level * jnp.repeat(jnp.exp(heights), dims[dim] // shards_of).reshape((-1,) + (1,) * (len(dims) - 1 - dim))
    return level


def assign_block(rng, own, number, rows, count, top, most, lean):
    sequence = jax.random.permutation(rng, count)
    packed, usual = portions_of(count, rows * top, most, lean, True), portions_of(count, rows * top, most, lean, False)
    places = jnp.arange(count)

    def named(sizes, rotation):
        used = int((sizes > 0).sum())
        fixed = max(1, used // 4)
        passed = fixed + (places - fixed + rotation * (used - fixed)) % max(1, count - fixed)
        return jnp.zeros((count,), jnp.int32).at[sequence[jnp.where(places < fixed, places, passed)]].set(jnp.asarray(sizes, jnp.int32))

    sizes = jnp.where(number % 4 == 0, named(packed, number // 4), named(usual, number - number // 4 - 1))
    mixed = jax.random.permutation(jax.random.fold_in(own, 3), count)
    donor, taker = mixed[0:count // 2 * 2:2], mixed[1:count // 2 * 2:2]
    room = jnp.minimum(sizes[donor] - 1, most - sizes[taker]) // 2
    room = jnp.where((donor == sequence[0]) | (taker == sequence[0]) | (sizes[taker] == 0), 0, jnp.maximum(room, 0))
    passed = jax.random.randint(jax.random.fold_in(own, 4), (count // 2,), 0, 1 << 20) % (room + 1)
    sizes = sizes.at[donor].add(-passed).at[taker].add(passed)
    items = jnp.searchsorted(jnp.cumsum(sizes), jnp.arange(rows * top), side="right").astype(jnp.int32)
    listing = items.reshape(top, rows).T
    listing = listing[jax.random.permutation(jax.random.fold_in(own, 1), rows)]
    rotation = jax.random.randint(jax.random.fold_in(own, 2), (rows, 1), 0, top)
    return jnp.take_along_axis(listing, (jnp.arange(top)[None, :] + rotation) % top, axis=1)


def portions_of(amount, total, limit, lean, full):
    loads = [(1 << 20) // math.isqrt(standing ** lean) + 1 for standing in range(1, amount + 1)]
    largest = limit if full else min(limit, max(-(-total // amount), total * loads[0] // sum(loads)))
    least = 1 if total - largest >= amount - 1 else 0
    given, rest = [largest] + [least] * (amount - 1), total - largest - least * (amount - 1)
    while rest > 0:
        free = [i for i in range(1, amount) if given[i] < largest] or [i for i in range(1, amount) if given[i] < limit]
        whole, remaining = sum([loads[i] for i in free]), rest
        for i in free:
            extra = min(limit - given[i], max(1, remaining * loads[i] // whole), rest)
            given[i] = given[i] + extra
            rest = rest - extra
    return np.array(given)


def centred(own_key, dims, width, limit, cuts=(), held_as=jnp.bfloat16):
    array = width * jax.random.normal(own_key, dims, jnp.float32)
    if cuts:
        array = array * steps_of(own_key, dims, cuts, -0.22, 0.18)
    return jnp.clip(array, -limit, limit).astype(held_as)


def setup_inputs(seed: int = 0) -> dict:
    seeds = jax.random.split(jax.random.key(seed), 8)
    tokens = centred(seeds[0], (TOKENS, D), 1.0, 6.0, ((0, 16),), jnp.float32)
    expert_ids_keys = jax.random.split(jax.random.fold_in(seeds[1], 1), TOKENS // TOK_DEV)
    expert_ids_turns = jax.random.permutation(jax.random.fold_in(seeds[1], 3), TOKENS // TOK_DEV)
    expert_ids = jax.vmap(lambda own, number: assign_block(jax.random.fold_in(seeds[1], 2), own, number, TOK_DEV, EXPERTS, TOP, CAP, 2))(expert_ids_keys, expert_ids_turns).reshape((TOKENS, TOP))
    gate_values = jnp.clip(jnp.exp(math.log(1.0) - 2.9957323 * jax.random.uniform(seeds[2], (TOKENS, TOP), jnp.float32) ** steps_of(seeds[2], (TOKENS, TOP), ((0, 16),), -0.2, 0.2)), 0.05, 1.0)
    valid_mask = draw_valid_mask(jax.random.fold_in(seeds[7], 71), 0)
    gate_weight = centred(seeds[4], (EXPERTS, FF, D), D ** -0.5, 0.125, ((0, 16), (1, 16)))
    up_weight = centred(seeds[5], (EXPERTS, FF, D), D ** -0.5, 0.125, ((0, 16), (1, 16)))
    down_weight = centred(seeds[6], (EXPERTS, FF, D), FF ** -0.5, 0.15625, ((0, 16), (1, 16)))
    return {"tokens": tokens, "expert_ids": expert_ids, "gate_values": gate_values, "valid_mask": valid_mask, "gate_weight": gate_weight, "up_weight": up_weight, "down_weight": down_weight}


def slot_ranks(flattened, expert_total):
    one_hot = (flattened[:, :, None] == jnp.arange(expert_total, dtype=jnp.int32)[None, None, :]).astype(jnp.int32)
    before = jnp.cumsum(one_hot, axis=1) - one_hot
    return jnp.sum(before * one_hot, axis=2).astype(jnp.int32)


def reference(tokens, expert_ids, gate_values, valid_mask, gate_weight, up_weight, down_weight):
    blocks = TOKENS // TOK_DEV
    flattened = expert_ids.reshape(blocks, TOK_DEV * TOP)
    slot_rank = slot_ranks(flattened, EXPERTS)
    block_index = jnp.arange(blocks, dtype=jnp.int32)[:, None]
    slot_place = ((flattened * blocks + block_index) * CAP + slot_rank).reshape(-1).astype(jnp.int32)
    token_rows = jnp.repeat(tokens.astype(jnp.bfloat16), TOP, axis=0)
    buffer = jnp.zeros((EXPERTS * blocks * CAP, D), jnp.bfloat16).at[slot_place].set(token_rows)
    buffer = buffer.reshape(EXPERTS, blocks * CAP, D)

    def run_expert(operands):
        expert_block, gate_matrix, up_matrix, down_matrix = operands
        rows = expert_block.astype(jnp.float32)
        gate_pre = jnp.dot(rows, gate_matrix.astype(jnp.float32).T, preferred_element_type=jnp.float32)
        up_pre = jnp.dot(rows, up_matrix.astype(jnp.float32).T, preferred_element_type=jnp.float32)
        hidden = (jax.nn.silu(gate_pre) * up_pre).astype(jnp.bfloat16)
        return jnp.dot(hidden.astype(jnp.float32), down_matrix.astype(jnp.float32), preferred_element_type=jnp.float32).astype(jnp.bfloat16)

    results = lax.map(run_expert, (buffer, gate_weight, up_weight, down_weight)).reshape(-1, D)
    places = slot_place.reshape(TOKENS, TOP)
    blended = jnp.zeros((TOKENS, D), jnp.float32)
    for choice_index in range(TOP):
        picked = results[places[:, choice_index]].astype(jnp.float32)
        blended = blended + gate_values[:, choice_index:choice_index + 1] * picked
    weights = valid_mask.astype(jnp.float32)
    blended = blended * weights[:, None]
    per_token = jnp.mean(blended * blended, axis=1)
    loss = jnp.sum(per_token * weights) / jnp.sum(weights)
    return blended, loss
```

```python
import jax
import jax.numpy as jnp
from jax import lax
from jax.sharding import PartitionSpec as P

SLOTS = 16


def on_device(tokens, expert_ids, gate_values, valid_mask, gate_weight, up_weight, down_weight):
    tok_count, width = tokens.shape
    local_experts = gate_weight.shape[0]
    blocks = lax.axis_size("expert")
    parts = lax.axis_size("dp")
    piece = width // parts
    me = lax.axis_index("expert")
    part = lax.axis_index("dp")
    weights = valid_mask.astype(jnp.float32)
    mine = lax.dynamic_slice(tokens, (0, part * piece), (tok_count, piece)).astype(jnp.bfloat16)
    column = lax.all_gather(mine, "expert", axis=0, tiled=True)
    every = lax.all_gather(column, "dp", axis=1, tiled=True)
    ids = lax.all_gather(expert_ids, "expert", axis=0, tiled=True)
    gates = lax.all_gather(gate_values * weights[:, None], "expert", axis=0, tiled=True)
    local = me * local_experts + jnp.arange(local_experts, dtype=jnp.int32)
    match = ids[:, None, :] == local[None, :, None]
    named = jnp.any(match, axis=2)
    gate = jnp.sum(jnp.where(match, gates[:, None, :], 0.0), axis=2).reshape(blocks, tok_count, local_experts)
    taken = named.astype(jnp.int32).reshape(blocks, tok_count, local_experts)
    rank = jnp.cumsum(taken, axis=1) - taken
    pick = (
        (rank.transpose(0, 2, 1)[:, :, None, :] == jnp.arange(SLOTS, dtype=jnp.int32)[None, None, :, None])
        & (taken.transpose(0, 2, 1)[:, :, None, :] > 0)
    )
    slot_gate = jnp.sum(jnp.where(pick, gate.transpose(0, 2, 1)[:, :, None, :], 0.0), axis=3)
    pick = pick.astype(jnp.bfloat16)
    rows = jnp.einsum(
        "best,btf->ebsf", pick, every.reshape(blocks, tok_count, width), preferred_element_type=jnp.float32
    ).astype(jnp.bfloat16)
    rows = rows.reshape(local_experts, blocks * SLOTS, width)
    gate_pre = jnp.einsum("erd,efd->erf", rows, gate_weight, preferred_element_type=jnp.float32)
    up_pre = jnp.einsum("erd,efd->erf", rows, up_weight, preferred_element_type=jnp.float32)
    hidden = (jax.nn.silu(gate_pre) * up_pre).astype(jnp.bfloat16)
    out = jnp.einsum("erf,efd->erd", hidden, down_weight, preferred_element_type=jnp.float32)
    out = out.reshape(local_experts, blocks, SLOTS, width) * slot_gate.transpose(1, 0, 2)[:, :, :, None]
    mixed = jnp.einsum(
        "best,ebsf->btf", pick, out.astype(jnp.bfloat16), preferred_element_type=jnp.float32
    ).reshape(blocks * tok_count, width)
    summed = lax.psum_scatter(mixed.astype(jnp.bfloat16), "dp", scatter_dimension=1, tiled=True)
    own = lax.psum_scatter(summed.astype(jnp.float32), "expert", scatter_dimension=0, tiled=True)
    blended = lax.all_gather(own, "dp", axis=1, tiled=True)
    per_token = jnp.mean(blended * blended, axis=1)
    local_loss = jnp.sum(per_token * weights)
    loss_sum, token_total = lax.psum((local_loss, jnp.sum(weights)), "expert")
    return (blended, loss_sum / token_total)


def solution(mesh):
    return jax.shard_map(
        on_device,
        mesh=mesh,
        in_specs=(
            P("expert", None),
            P("expert", None),
            P("expert", None),
            P("expert"),
            P("expert", "dp", None),
            P("expert", "dp", None),
            P("expert", "dp", None),
        ),
        out_specs=(P("expert", None), P()),
        check_vma=False,
    )
```

```python
import jax
import jax.numpy as jnp
from jax import lax
from jax.experimental import pallas as pl
from jax.experimental.pallas import tpu as pltpu
from jax.sharding import PartitionSpec as P

MESH = pl.DeviceIdType.MESH
BF = jnp.bfloat16
F32 = jnp.float32
SLOTS = 16
ORDER = (0, 1, 7, 2, 6, 3, 5, 4)
POS = {dz: k for k, dz in enumerate(ORDER)}
GROUPS = ((0, 1, 7, 2), (6, 3, 5, 4))
XFIRST = {0: False, 1: True, 7: False, 2: True, 6: False, 3: True, 5: False, 4: True}
TURN = {0: 1, 1: 1, 7: -1, 2: -1, 6: 1, 3: 1, 5: -1, 4: -1}


def kernel(tok, meta, mask, gw, uw, dw, out, loss,
           TOK, META, X, W1, WD, SEL, STR, GS, PART, PX, PEX, RB, RA, ACCB, SUMB, ACCA, Q, ZR, FIN, LR, LS,
           wsem, zs, zr, ms, mr, as_, ar, bs, br, ps, pr, qs, qr, rbs, rbr, ras, rar, vs, vr, fs, fr, ls, lr):
    dp = lax.axis_index("dp")
    ex = lax.axis_index("expert")
    y, x = dp // 4, dp % 4
    z, c = ex // 2, ex % 2

    def peer(dz, rc):
        core = c if rc == 0 else 1 - c
        return {"dp": dp, "expert": ((z + dz) % 8) * 2 + core}

    def step(axis, d):
        if axis == "x":
            return {"dp": y * 4 + (x + d + 4) % 4, "expert": ex}
        return {"dp": ((y + d + 4) % 4) * 4 + x, "expert": ex}

    def remote(src, dst, ssem, rsem, dev):
        return pltpu.make_async_remote_copy(
            src_ref=src, dst_ref=dst, send_sem=ssem, recv_sem=rsem, device_id=dev, device_id_type=MESH)

    pending = []

    def send(src, dst, ssem, rsem, dev):
        cp = remote(src, dst, ssem, rsem, dev)
        cp.start()
        pending.append(cp)

    def arrive(dst, ssem, rsem):
        remote(dst, dst, ssem, rsem, peer(0, 1)).wait_recv()

    weights = [
        pltpu.make_async_copy(gw, W1.at[:, pl.ds(0, 96), :], wsem.at[0]),
        pltpu.make_async_copy(uw, W1.at[:, pl.ds(128, 96), :], wsem.at[1]),
        pltpu.make_async_copy(dw, WD.at[:, pl.ds(0, 96), :], wsem.at[2]),
    ]
    for w in weights:
        w.start()

    barrier = pltpu.get_barrier_semaphore()
    everyone = [peer(dz, rc) for dz in range(8) for rc in range(2) if (dz, rc) != (0, 0)]
    everyone += [step(axis, d) for axis in "xy" for d in (1, 2, 3)]
    for dev in everyone:
        pl.semaphore_signal(barrier, inc=1, device_id=dev, device_id_type=MESH)

    for i in range(4):
        for j in range(4):
            f = (i * 4 + j) * 128
            TOK[0, 0, i, j] = tok[:, f:f + 128].astype(BF)
    META[0] = meta[...]
    pl.semaphore_wait(barrier, len(everyone))

    for n, dz in enumerate(ORDER[1:]):
        back = (8 - dz) % 8
        send(TOK.at[0, 0, y, x], TOK.at[back, 0, y, x], zs.at[dz], zr.at[back], peer(dz, 0))
    for dz in ORDER:
        back = (8 - dz) % 8
        for rc in range(2):
            if (dz, rc) != (0, 0):
                k, kb = 2 * POS[dz] + rc, 2 * POS[back] + rc
                send(meta, META.at[kb], ms.at[k], mr.at[kb], peer(dz, rc))
    send(TOK.at[0, 0], TOK.at[0, 1], ps.at[0], pr.at[0], peer(0, 1))

    zero = jnp.zeros((32, 2048), BF)
    for e in range(8):
        W1[e, 96:128, :] = zero
        W1[e, 224:256, :] = zero
        WD[e, 96:128, :] = zero

    def near(dz):
        return ("x", "y", x, y) if XFIRST[dz] else ("y", "x", y, x)

    def piece(ref, dz, pos):
        pos = (pos + 4) % 4
        return ref.at[dz, 0, y, pos] if XFIRST[dz] else ref.at[dz, 0, pos, x]

    def bundle(ref, dz, pos):
        pos = (pos + 4) % 4
        return ref.at[dz, 0, pos] if XFIRST[dz] else ref.at[dz, 0, :, pos]

    def spread(part, dz, axis, me, ssem, rsem):
        send(part(TOK, dz, me), part(TOK, dz, me), ssem.at[dz, 0], rsem.at[dz, 0], step(axis, 1))
        send(part(TOK, dz, me), part(TOK, dz, me), ssem.at[dz, 1], rsem.at[dz, 1], step(axis, -1))

    def onward(part, dz, axis, me, ssem, rsem):
        s = TURN[dz]
        got = part(TOK, dz, me - s)
        arrive(got, ssem.at[dz, 2], rsem.at[dz, 0 if s == 1 else 1])
        send(got, got, ssem.at[dz, 2], rsem.at[dz, 2], step(axis, s))

    def complete(part, dz, me, ssem, rsem):
        s = TURN[dz]
        arrive(part(TOK, dz, me + s), ssem.at[dz, 2], rsem.at[dz, 1 if s == 1 else 0])
        arrive(part(TOK, dz, me + 2), ssem.at[dz, 2], rsem.at[dz, 2])

    rest = ORDER[1:]
    for dz in rest:
        a, b, ma, mb = near(dz)
        arrive(TOK.at[dz, 0, y, x], zs.at[0], zr.at[dz])
        spread(piece, dz, a, ma, as_, ar)
    for dz in rest:
        a, b, ma, mb = near(dz)
        onward(piece, dz, a, ma, as_, ar)
    for dz in rest:
        a, b, ma, mb = near(dz)
        complete(piece, dz, ma, as_, ar)
        spread(bundle, dz, b, mb, bs, br)

    for k in range(1, 16):
        arrive(META.at[k], ms.at[0], mr.at[k])
    row = lax.broadcasted_iota(jnp.int32, (128, 128), 0)
    col = lax.broadcasted_iota(jnp.int32, (128, 128), 1)
    before = (row < col).astype(F32).astype(BF)
    local = (lax.broadcasted_iota(jnp.int32, (8, 128), 0) + ex * 8).astype(F32)
    slot = lax.broadcasted_iota(jnp.int32, (8, SLOTS, 128), 1).astype(F32)

    def route(k, carry):
        m = META[k]
        named = jnp.zeros((8, 128), F32)
        gate = jnp.zeros((8, 128), F32)
        for i in range(8):
            hit = m[i:i + 1, :] == local
            named = jnp.where(hit, 1.0, named)
            gate = gate + jnp.where(hit, m[8 + i:9 + i, :], 0.0)
        rank = jnp.dot(named.astype(BF), before, preferred_element_type=F32)
        rank = jnp.where(named > 0.0, rank, -1.0)
        pick = jnp.broadcast_to(rank[:, None, :], (8, SLOTS, 128)) == slot
        one = jnp.where(pick, 1.0, 0.0).reshape(128, 128)
        SEL[k] = one.astype(BF)
        STR[k] = one.T.astype(BF)
        held = jnp.where(pick, jnp.broadcast_to(gate[:, None, :], (8, SLOTS, 128)), 0.0)
        GS[:, pl.ds(pl.multiple_of(k * SLOTS, SLOTS), SLOTS), :] = jnp.broadcast_to(
            jnp.sum(held, axis=2, keepdims=True), (8, SLOTS, 128))
        return carry

    lax.fori_loop(0, 16, route, 0)

    for dz in rest:
        a, b, ma, mb = near(dz)
        onward(bundle, dz, b, mb, bs, br)
    for dz in rest:
        a, b, ma, mb = near(dz)
        complete(bundle, dz, mb, bs, br)
        send(TOK.at[dz, 0], TOK.at[dz, 1], ps.at[dz], pr.at[dz], peer(0, 1))

    for w in weights:
        w.wait()

    def select(dz, rc):
        k = 2 * POS[dz] + rc
        pick = SEL[k]
        for i in range(4):
            rhs = jnp.concatenate([TOK[dz, rc, i, j] for j in range(4)], axis=1)
            got = jnp.dot(pick, rhs, preferred_element_type=F32).astype(BF)
            X[:, k * SLOTS:(k + 1) * SLOTS, i * 512:(i + 1) * 512] = got.reshape(8, SLOTS, 512)

    def ffn(group):
        lo = 2 * SLOTS * POS[group[0]]
        hi = lo + 2 * SLOTS * len(group)

        def one(e, carry):
            pre = lax.dot_general(X[e, lo:hi, :], W1[e], (((1,), (1,)), ((), ())), preferred_element_type=F32)
            g, u = pre[:, :128], pre[:, 128:]
            h = (g / (1.0 + jnp.exp(-g)) * u).astype(BF)
            scale = GS[e, lo:hi, :]
            scale = jnp.concatenate([scale] * 4, axis=1)
            for i in range(4):
                o = jnp.dot(h, WD[e, :, i * 512:(i + 1) * 512], preferred_element_type=F32)
                X[e, lo:hi, i * 512:(i + 1) * 512] = (o * scale).astype(BF)
            return carry

        lax.fori_loop(0, 8, one, 0)

    def combine(dz, rc, i):
        k = 2 * POS[dz] + rc
        rhs = X[:, k * SLOTS:(k + 1) * SLOTS, i * 512:(i + 1) * 512].reshape(128, 512)
        return jnp.dot(STR[k], rhs, preferred_element_type=F32)

    def home(ref, dz, pos):
        pos = (pos + 4) % 4
        return ref.at[dz, pos] if XFIRST[dz] else ref.at[dz, :, pos]

    for group in GROUPS:
        for dz in group:
            select(dz, 0)
        for dz in group:
            arrive(TOK.at[dz, 1], ps.at[0], pr.at[dz])
            select(dz, 1)
        ffn(group)
        for dz in group:
            for i in range(4):
                got = combine(dz, 1, i).astype(BF)
                for j in range(4):
                    PX[dz, i, j] = got[:, j * 128:(j + 1) * 128]
            send(PX.at[dz], PEX.at[dz], qs.at[dz], qr.at[dz], peer(0, 1))
        for dz in group:
            a, b, ma, mb = near(dz)
            s = TURN[dz]
            arrive(PEX.at[dz], qs.at[dz], qr.at[dz])
            for i in range(4):
                got = combine(dz, 0, i)
                for j in range(4):
                    PART[dz, i, j] = (got[:, j * 128:(j + 1) * 128] + PEX[dz, i, j].astype(F32)).astype(BF)
            send(home(PART, dz, mb + 2), RB.at[dz, 0], rbs.at[dz, 0], rbr.at[dz, 0], step(b, s))
            send(home(PART, dz, mb - s), RB.at[dz, 1], rbs.at[dz, 1], rbr.at[dz, 1], step(b, -s))

    for dz in ORDER:
        a, b, ma, mb = near(dz)
        s = TURN[dz]
        arrive(RB.at[dz, 0], rbs.at[dz, 0], rbr.at[dz, 0])
        ACCB[dz] = (RB[dz, 0].astype(F32) + home(PART, dz, mb + s)[...].astype(F32)).astype(BF)
        send(ACCB.at[dz], RB.at[dz, 2], rbs.at[dz, 2], rbr.at[dz, 2], step(b, s))
    for dz in ORDER:
        a, b, ma, mb = near(dz)
        s = TURN[dz]
        arrive(RB.at[dz, 1], rbs.at[dz, 1], rbr.at[dz, 1])
        arrive(RB.at[dz, 2], rbs.at[dz, 2], rbr.at[dz, 2])
        SUMB[dz] = (home(PART, dz, mb)[...].astype(F32) + RB[dz, 1].astype(F32) + RB[dz, 2].astype(F32)).astype(BF)
        send(SUMB.at[dz, (ma + 2) % 4], RA.at[dz, 0], ras.at[dz, 0], rar.at[dz, 0], step(a, s))
        send(SUMB.at[dz, (ma - s + 4) % 4], RA.at[dz, 1], ras.at[dz, 1], rar.at[dz, 1], step(a, -s))
    for dz in ORDER:
        a, b, ma, mb = near(dz)
        s = TURN[dz]
        arrive(RA.at[dz, 0], ras.at[dz, 0], rar.at[dz, 0])
        ACCA[dz] = (RA[dz, 0].astype(F32) + SUMB[dz, (ma + s + 4) % 4].astype(F32)).astype(BF)
        send(ACCA.at[dz], RA.at[dz, 2], ras.at[dz, 2], rar.at[dz, 2], step(a, s))
    for dz in ORDER[1:] + ORDER[:1]:
        a, b, ma, mb = near(dz)
        arrive(RA.at[dz, 1], ras.at[dz, 1], rar.at[dz, 1])
        arrive(RA.at[dz, 2], ras.at[dz, 2], rar.at[dz, 2])
        total = SUMB[dz, ma].astype(F32) + RA[dz, 1].astype(F32) + RA[dz, 2].astype(F32)
        if dz:
            Q[dz] = total.astype(BF)
            back = (8 - dz) % 8
            send(Q.at[dz], ZR.at[back], vs.at[dz], vr.at[back], peer(dz, 0))
    for dz in ORDER[1:]:
        arrive(ZR.at[dz], vs.at[0], vr.at[dz])
        total = total + ZR[dz].astype(F32)
    FIN[y, x] = total.astype(BF)

    for d in (1, 3, 2):
        send(FIN.at[y, x], FIN.at[y, x], fs.at[d], fr.at[d], step("x", d))
    for d in (1, 3, 2):
        arrive(FIN.at[y, (x - d + 4) % 4], fs.at[0], fr.at[d])
    for d in (1, 3, 2):
        send(FIN.at[y], FIN.at[y], fs.at[4 + d], fr.at[4 + d], step("y", d))
    for d in (1, 3, 2):
        arrive(FIN.at[(y - d + 4) % 4], fs.at[0], fr.at[4 + d])

    squares = jnp.zeros((8, 128), F32)
    for i in range(4):
        for j in range(4):
            v = FIN[i, j]
            f = (i * 4 + j) * 128
            out[:, f:f + 128] = v
            w = v.astype(F32)
            squares = squares + jnp.sum((w * w).reshape(16, 8, 128), axis=0)
    LS[0:8] = squares
    LS[8:16] = mask[...]
    for dz in ORDER:
        back = (8 - dz) % 8
        for rc in range(2):
            if (dz, rc) != (0, 0):
                k, kb = 2 * POS[dz] + rc, 2 * POS[back] + rc
                send(LS, LR.at[kb], ls.at[k], lr.at[kb], peer(dz, rc))
    LR[0] = LS[...]
    for k in range(1, 16):
        arrive(LR.at[k], ls.at[0], lr.at[k])
    gathered = jnp.sum(LR[...], axis=0)
    top = jnp.sum(jnp.sum(gathered[0:8], axis=0, keepdims=True), axis=1, keepdims=True) * (1.0 / 2048.0)
    count = jnp.sum(jnp.sum(gathered[8:16], axis=0, keepdims=True), axis=1, keepdims=True)
    loss[...] = jnp.broadcast_to(top / count, (8, 128))

    for cp in pending:
        cp.wait_send()


def on_device(tokens, expert_ids, gate_values, valid_mask, gate_weight, up_weight, down_weight):
    weights = valid_mask.astype(F32)
    meta = jnp.concatenate([expert_ids.astype(F32).T, (gate_values * weights[:, None]).T], axis=0)
    mask = jnp.concatenate([weights[None, :], jnp.zeros((7, 128), F32)], axis=0)
    vmem = pl.BlockSpec(memory_space=pltpu.VMEM)
    hbm = pl.BlockSpec(memory_space=pl.ANY)
    dma = pltpu.SemaphoreType.DMA
    out, loss = pl.pallas_call(
        kernel,
        out_shape=(jax.ShapeDtypeStruct((128, 2048), BF), jax.ShapeDtypeStruct((8, 128), F32)),
        in_specs=[vmem, vmem, vmem, hbm, hbm, hbm],
        out_specs=(vmem, vmem),
        scratch_shapes=[
            pltpu.VMEM((8, 2, 4, 4, 128, 128), BF),
            pltpu.VMEM((16, 16, 128), F32),
            pltpu.VMEM((8, 256, 2048), BF),
            pltpu.VMEM((8, 256, 2048), BF),
            pltpu.VMEM((8, 128, 2048), BF),
            pltpu.VMEM((16, 128, 128), BF),
            pltpu.VMEM((16, 128, 128), BF),
            pltpu.VMEM((8, 256, 128), F32),
            pltpu.VMEM((8, 4, 4, 128, 128), BF),
            pltpu.VMEM((8, 4, 4, 128, 128), BF),
            pltpu.VMEM((8, 4, 4, 128, 128), BF),
            pltpu.VMEM((8, 3, 4, 128, 128), BF),
            pltpu.VMEM((8, 3, 128, 128), BF),
            pltpu.VMEM((8, 4, 128, 128), BF),
            pltpu.VMEM((8, 4, 128, 128), BF),
            pltpu.VMEM((8, 128, 128), BF),
            pltpu.VMEM((8, 128, 128), BF),
            pltpu.VMEM((8, 128, 128), BF),
            pltpu.VMEM((4, 4, 128, 128), BF),
            pltpu.VMEM((16, 16, 128), F32),
            pltpu.VMEM((16, 128), F32),
            dma((3,)), dma((8,)), dma((8,)), dma((16,)), dma((16,)),
            dma((8, 3)), dma((8, 3)), dma((8, 3)), dma((8, 3)),
            dma((8,)), dma((8,)), dma((8,)), dma((8,)),
            dma((8, 3)), dma((8, 3)), dma((8, 3)), dma((8, 3)),
            dma((8,)), dma((8,)), dma((8,)), dma((8,)), dma((16,)), dma((16,)),
        ],
        compiler_params=pltpu.CompilerParams(
            collective_id=0, has_side_effects=True, vmem_limit_bytes=62 * 1024 * 1024),
    )(tokens, meta, mask, gate_weight, up_weight, down_weight)
    return out.astype(F32), loss[0, 0]


def solution(mesh):
    return jax.shard_map(
        on_device,
        mesh=mesh,
        in_specs=(
            P("expert", None),
            P("expert", None),
            P("expert", None),
            P("expert"),
            P("expert", "dp", None),
            P("expert", "dp", None),
            P("expert", "dp", None),
        ),
        out_specs=(P("expert", None), P()),
        check_vma=False,
    )
```

```python
import jax
import jax.numpy as jnp
from jax import lax
from jax.experimental import pallas as pl
from jax.experimental.pallas import tpu as pltpu
from jax.sharding import PartitionSpec as P

MESH = pl.DeviceIdType.MESH
BF = jnp.bfloat16
F32 = jnp.float32
SLOTS = 16
ORDER = (0, 2, 6, 3, 5, 4, 1, 7)
POS = {dz: k for k, dz in enumerate(ORDER)}
GZ, G0, G1 = (0,), (2, 6, 3, 5), (4, 1, 7)
PLANE = (2, 6, 3, 5, 4)
XFIRST = {0: False, 2: True, 6: False, 3: True, 5: False, 4: True, 1: False, 7: True}


def kernel(ids, gates, mask, tok, gw, uw, dw, out, loss,
           TOKF, TOK, MINE, META, X, H, W1, WD, SEL, STR, GS, PART, PX, PEX, RB, RA, ACCB, SUMB, Q, ZR, FIN, LS, LR, LT, LX, LY,
           wsem, zs, zr, ms, mr, as_, ar, bs, br, ps, pr, qs, qr, rbs, rbr, ras, rar, vs, vr, fs, fr, ls, lr):
    dp = lax.axis_index("dp")
    ex = lax.axis_index("expert")
    y, x = dp // 4, dp % 4
    z, c = ex // 2, ex % 2

    def peer(dz, rc):
        core = c if rc == 0 else 1 - c
        return {"dp": dp, "expert": ((z + dz) % 8) * 2 + core}

    def step(axis, d):
        if axis == "x":
            return {"dp": y * 4 + (x + d + 4) % 4, "expert": ex}
        return {"dp": ((y + d + 4) % 4) * 4 + x, "expert": ex}

    def remote(src, dst, ssem, rsem, dev):
        return pltpu.make_async_remote_copy(
            src_ref=src, dst_ref=dst, send_sem=ssem, recv_sem=rsem, device_id=dev, device_id_type=MESH)

    pending = []

    def send(src, dst, ssem, rsem, dev):
        cp = remote(src, dst, ssem, rsem, dev)
        cp.start()
        pending.append(cp)

    def arrive(dst, ssem, rsem):
        remote(dst, dst, ssem, rsem, peer(0, 1)).wait_recv()

    load = pltpu.make_async_copy(tok, TOKF, wsem.at[3])
    load.start()

    barrier = pltpu.get_barrier_semaphore()
    everyone = [peer(dz, rc) for dz in range(8) for rc in range(2) if (dz, rc) != (0, 0)]
    everyone += [step(axis, d) for axis in "xy" for d in (1, 2, 3)]
    for dev in everyone:
        pl.semaphore_signal(barrier, inc=1, device_id=dev, device_id_type=MESH)

    weights = [
        pltpu.make_async_copy(gw, W1.at[:, pl.ds(0, 96), :], wsem.at[0]),
        pltpu.make_async_copy(uw, W1.at[:, pl.ds(128, 96), :], wsem.at[1]),
        pltpu.make_async_copy(dw, WD.at[:, pl.ds(0, 96), :], wsem.at[2]),
    ]

    valid = jnp.broadcast_to(mask[...], (8, 128)) > 0
    MINE[0:8] = jnp.where(valid, ids[...], -1).astype(F32)
    MINE[8:16] = gates[...]
    META[0] = MINE[...]

    load.wait()
    for w in weights:
        w.start()
    for i in range(4):
        for j in range(4):
            f = (i * 4 + j) * 128
            TOK[0, 0, i, j] = TOKF[:, f:f + 128].astype(BF)
    pl.semaphore_wait(barrier, len(everyone))

    def back(dz):
        return (8 - dz) % 8

    def meta(dz):
        send(MINE, META.at[2 * POS[back(dz)]], ms.at[dz], mr.at[2 * POS[back(dz)]], peer(dz, 0))

    def slice_to(dz):
        send(TOK.at[0, 0, y, x], TOK.at[back(dz), 0, y, x], zs.at[dz], zr.at[back(dz)], peer(dz, 0))

    send(MINE, META.at[1], ms.at[0], mr.at[1], peer(0, 1))
    slice_to(2)
    slice_to(6)
    send(TOK.at[0, 0], TOK.at[0, 1], ps.at[0], pr.at[0], peer(0, 1))
    for dz in PLANE[2:]:
        slice_to(dz)
    for dz in ORDER[1:]:
        meta(dz)

    def whole():
        send(TOK.at[0, 0], TOK.at[7, 0], zs.at[1], zr.at[7], peer(1, 0))
        send(TOK.at[0, 0], TOK.at[1, 0], zs.at[7], zr.at[1], peer(7, 0))

    zero = jnp.zeros((32, 2048), BF)
    for e in range(8):
        W1[e, 96:128, :] = zero
        W1[e, 224:256, :] = zero
        WD[e, 96:128, :] = zero

    def near(dz):
        return ("x", "y", x, y) if XFIRST[dz] else ("y", "x", y, x)

    def wrap(pos):
        return (pos + 8) % 4

    def piece(dz, pos):
        return TOK.at[dz, 0, y, wrap(pos)] if XFIRST[dz] else TOK.at[dz, 0, wrap(pos), x]

    def bundle_half(dz, pos, h):
        two = pl.ds(2 * h, 2)
        return TOK.at[dz, 0, wrap(pos), two] if XFIRST[dz] else TOK.at[dz, 0, two, wrap(pos)]

    def t1(dz):
        a, b, ma, mb = near(dz)
        arrive(TOK.at[dz, 0, y, x], zs.at[dz], zr.at[dz])
        for d in (2, 1, 3):
            send(piece(dz, ma), piece(dz, ma), as_.at[dz, d - 1], ar.at[dz, d - 1], step(a, d))

    def t3(dz):
        a, b, ma, mb = near(dz)
        for d in (1, 3, 2):
            arrive(piece(dz, ma - d), as_.at[dz, d - 1], ar.at[dz, d - 1])
        for n, h, d in ((0, 0, 1), (1, 1, -1), (2, 1, 1), (3, 0, -1)):
            send(bundle_half(dz, mb, h), bundle_half(dz, mb, h), bs.at[dz, n], br.at[dz, n], step(b, d))

    def t4(dz):
        a, b, ma, mb = near(dz)
        for n, h, d in ((0, 0, 1), (1, 1, -1)):
            got = bundle_half(dz, mb - d, h)
            arrive(got, bs.at[dz, n], br.at[dz, n])
            send(got, got, bs.at[dz, 4 + n], br.at[dz, 4 + n], step(b, d))

    def t5(dz):
        a, b, ma, mb = near(dz)
        if dz in PLANE:
            for n, h, d in ((2, 1, 1), (3, 0, -1), (4, 0, 2), (5, 1, -2)):
                arrive(bundle_half(dz, mb - d, h), bs.at[dz, n], br.at[dz, n])
        else:
            arrive(TOK.at[dz, 0], zs.at[dz], zr.at[dz])
        send(TOK.at[dz, 0], TOK.at[dz, 1], ps.at[dz], pr.at[dz], peer(0, 1))

    row = lax.broadcasted_iota(jnp.int32, (128, 128), 0)
    col = lax.broadcasted_iota(jnp.int32, (128, 128), 1)
    before = (row < col).astype(F32).astype(BF)
    local = (lax.broadcasted_iota(jnp.int32, (8, 128), 0) + ex * 8).astype(F32)
    slot = lax.broadcasted_iota(jnp.int32, (8, SLOTS, 128), 1).astype(F32)

    def route(k, carry):
        m = META[k]
        named = jnp.zeros((8, 128), F32)
        gate = jnp.zeros((8, 128), F32)
        for i in range(8):
            hit = m[i:i + 1, :] == local
            named = jnp.where(hit, 1.0, named)
            gate = gate + jnp.where(hit, m[8 + i:9 + i, :], 0.0)
        rank = jnp.dot(named.astype(BF), before, preferred_element_type=F32)
        rank = jnp.where(named > 0.0, rank, -1.0)
        pick = jnp.broadcast_to(rank[:, None, :], (8, SLOTS, 128)) == slot
        one = jnp.where(pick, 1.0, 0.0).reshape(128, 128)
        SEL[k] = one.astype(BF)
        STR[k] = one.T.astype(BF)
        held = jnp.where(pick, jnp.broadcast_to(gate[:, None, :], (8, SLOTS, 128)), 0.0)
        GS[:, pl.ds(pl.multiple_of(k * SLOTS, SLOTS), SLOTS), :] = jnp.broadcast_to(
            jnp.sum(held, axis=2, keepdims=True), (8, SLOTS, 128))
        return carry

    def metas():
        for dz in ORDER[1:]:
            arrive(META.at[2 * POS[dz]], ms.at[dz], mr.at[2 * POS[dz]])
        for dz in ORDER[1:]:
            k = 2 * POS[dz]
            send(META.at[k], META.at[k + 1], ms.at[8 + dz], mr.at[k + 1], peer(0, 1))
        for dz in ORDER[1:]:
            k = 2 * POS[dz]
            arrive(META.at[k + 1], ms.at[8 + dz], mr.at[k + 1])
        lax.fori_loop(2, 16, route, 0)

    def own_plane():
        arrive(META.at[1], ms.at[0], mr.at[1])
        lax.fori_loop(0, 2, route, 0)

    def select(dz, rc):
        if rc:
            arrive(TOK.at[dz, 1], ps.at[dz], pr.at[dz])
        k = 2 * POS[dz] + rc
        pick = SEL[k]
        for i in range(4):
            rhs = jnp.concatenate([TOK[dz, rc, i, j] for j in range(4)], axis=1)
            got = jnp.dot(pick, rhs, preferred_element_type=F32).astype(BF)
            X[:, k * SLOTS:(k + 1) * SLOTS, i * 512:(i + 1) * 512] = got.reshape(8, SLOTS, 512)

    def span(group):
        lo = 2 * SLOTS * POS[group[0]]
        return lo, lo + 2 * SLOTS * len(group)

    def ups(group, first, last):
        lo, hi = span(group)

        def one(e, carry):
            pre = lax.dot_general(X[e, lo:hi, :], W1[e], (((1,), (1,)), ((), ())), preferred_element_type=F32)
            g, u = pre[:, :128], pre[:, 128:]
            H[e, lo:hi, :] = (g / (1.0 + jnp.exp(-g)) * u).astype(BF)
            return carry

        lax.fori_loop(first, last, one, 0, unroll=2)

    def downs(group, first, last):
        lo, hi = span(group)

        def one(e, carry):
            h = H[e, lo:hi, :]
            scale = GS[e, lo:hi, :]
            scale = jnp.concatenate([scale] * 4, axis=1)
            for i in range(4):
                o = jnp.dot(h, WD[e, :, i * 512:(i + 1) * 512], preferred_element_type=F32)
                X[e, lo:hi, i * 512:(i + 1) * 512] = (o * scale).astype(BF)
            return carry

        lax.fori_loop(first, last, one, 0, unroll=2)

    def combine(dz, rc, i):
        k = 2 * POS[dz] + rc
        rhs = X[:, k * SLOTS:(k + 1) * SLOTS, i * 512:(i + 1) * 512].reshape(128, 512)
        return jnp.dot(STR[k], rhs, preferred_element_type=F32)

    def give(dz):
        for i in range(4):
            got = combine(dz, 1, i).astype(BF)
            for j in range(4):
                PX[dz, i, j] = got[:, j * 128:(j + 1) * 128]
        send(PX.at[dz], PEX.at[dz], qs.at[dz], qr.at[dz], peer(0, 1))

    def home(dz, pos, h):
        two = pl.ds(2 * h, 2)
        return PART.at[dz, wrap(pos), two] if XFIRST[dz] else PART.at[dz, two, wrap(pos)]

    def plus(*refs):
        total = refs[0][...].astype(F32)
        for ref in refs[1:]:
            total = total + ref[...].astype(F32)
        return total

    def r1(dz):
        a, b, ma, mb = near(dz)
        arrive(PEX.at[dz], qs.at[dz], qr.at[dz])
        for i in range(4):
            got = combine(dz, 0, i)
            for j in range(4):
                PART[dz, i, j] = (got[:, j * 128:(j + 1) * 128] + PEX[dz, i, j].astype(F32)).astype(BF)
        send(home(dz, mb + 2, 0), RB.at[dz, 0], rbs.at[dz, 0], rbr.at[dz, 0], step(b, 1))
        send(home(dz, mb + 2, 1), RB.at[dz, 1], rbs.at[dz, 1], rbr.at[dz, 1], step(b, -1))
        send(home(dz, mb - 1, 0), RB.at[dz, 3], rbs.at[dz, 3], rbr.at[dz, 3], step(b, -1))
        send(home(dz, mb + 1, 1), RB.at[dz, 4], rbs.at[dz, 4], rbr.at[dz, 4], step(b, 1))

    def r2(dz):
        a, b, ma, mb = near(dz)
        for n, d in ((0, 1), (1, -1)):
            arrive(RB.at[dz, n], rbs.at[dz, n], rbr.at[dz, n])
            ACCB[dz, n] = plus(RB.at[dz, n], home(dz, mb + d, n)).astype(BF)
        for n, d, m in ((0, 1, 2), (1, -1, 5)):
            send(ACCB.at[dz, n], RB.at[dz, m], rbs.at[dz, m], rbr.at[dz, m], step(b, d))

    def r3(dz):
        a, b, ma, mb = near(dz)
        for n in (3, 4, 2, 5):
            arrive(RB.at[dz, n], rbs.at[dz, n], rbr.at[dz, n])
        SUMB[dz, 0:2] = plus(home(dz, mb, 0), RB.at[dz, 2], RB.at[dz, 3]).astype(BF)
        SUMB[dz, 2:4] = plus(home(dz, mb, 1), RB.at[dz, 4], RB.at[dz, 5]).astype(BF)
        for d in (2, 1, 3):
            send(SUMB.at[dz, wrap(ma + d)], RA.at[dz, d - 1], ras.at[dz, d - 1], rar.at[dz, d - 1], step(a, d))

    def r5(dz):
        a, b, ma, mb = near(dz)
        for d in (1, 3, 2):
            arrive(RA.at[dz, d - 1], ras.at[dz, d - 1], rar.at[dz, d - 1])
        Q[dz] = plus(SUMB.at[dz, ma], RA.at[dz, 0], RA.at[dz, 1], RA.at[dz, 2])
        if dz:
            ZR[8 + dz] = Q[dz].astype(BF)
            send(ZR.at[8 + dz], ZR.at[back(dz)], vs.at[dz], vr.at[back(dz)], peer(dz, 0))

    def each(task, group):
        for dz in group:
            task(dz)


    own_plane()
    select(0, 0)
    each(t1, (2, 6))
    select(0, 1)
    for w in weights:
        w.wait()
    ups(GZ, 0, 4)
    each(t1, (3, 5))
    each(t3, (2, 6))
    ups(GZ, 4, 8)
    t1(4)
    whole()
    each(t4, (2, 6))
    each(t3, (3, 5))
    downs(GZ, 0, 8)
    give(0)
    metas()
    each(t5, (2, 6))
    each(t4, (3, 5))
    t3(4)
    r1(0)
    select(2, 0)
    select(6, 0)
    each(t5, (3, 5))
    select(2, 1)
    select(6, 1)
    t4(4)
    r2(0)
    select(3, 0)
    select(5, 0)
    select(3, 1)
    select(5, 1)
    ups(G0, 0, 4)
    t5(4)
    r3(0)
    ups(G0, 4, 8)
    downs(G0, 0, 8)
    each(give, G0)
    each(t5, (1, 7))
    select(4, 0)
    select(4, 1)
    select(1, 0)
    select(7, 0)
    each(r1, G0)
    select(1, 1)
    select(7, 1)
    r5(0)
    ups(G1, 0, 4)
    each(r2, G0)
    ups(G1, 4, 8)
    downs(G1, 0, 4)
    each(r3, G0)
    downs(G1, 4, 8)
    each(give, G1)
    each(r5, G0)
    each(r1, G1)
    each(r2, G1)
    each(r3, G1)
    each(r5, G1)
    total = Q[0]
    for dz in ORDER[1:]:
        arrive(ZR.at[dz], vs.at[dz], vr.at[dz])
        total = total + ZR[dz].astype(F32)
    FIN[0, y, x] = total[0:64].astype(BF)
    FIN[1, y, x] = total[64:128].astype(BF)

    def strip(h, first, pos):
        if first:
            return FIN.at[0, y, wrap(pos)] if h == 0 else FIN.at[1, wrap(pos), x]
        return FIN.at[0, wrap(pos)] if h == 0 else FIN.at[1, :, wrap(pos)]

    for first in (True, False):
        base = 0 if first else 8
        legs = (("x", x), ("y", y)) if first else (("y", y), ("x", x))
        for d in (1, 3, 2):
            for h, (axis, me) in enumerate(legs):
                n = base + 4 * h + d
                send(strip(h, first, me), strip(h, first, me), fs.at[n], fr.at[n], step(axis, d))
        if first:
            LS[...] = jnp.sum((total * total).reshape(16, 8, 128), axis=0)
            for dz in ORDER:
                for rc in range(2):
                    if (dz, rc) != (0, 0):
                        k, kb = 2 * POS[dz] + rc, 2 * POS[back(dz)] + rc
                        send(LS, LR.at[kb], ls.at[k], lr.at[kb], peer(dz, rc))
            LR[0] = LS[...]
        for d in (1, 3, 2):
            for h, (axis, me) in enumerate(legs):
                n = base + 4 * h + d
                arrive(strip(h, first, me - d), fs.at[n], fr.at[n])
        if first:
            continue

    for k in range(1, 16):
        arrive(LR.at[k], ls.at[k], lr.at[k])
    LT[0] = jnp.sum(LR[...], axis=0)
    for d in (1, 3, 2):
        send(LT.at[0], LX.at[d], ls.at[16 + d], lr.at[16 + d], step("x", d))
    for i in range(4):
        for j in range(4):
            f = (i * 4 + j) * 128
            out[0:64, f:f + 128] = FIN[0, i, j].astype(out.dtype)
            out[64:128, f:f + 128] = FIN[1, i, j].astype(out.dtype)
    LX[0] = LT[0]
    for d in (1, 3, 2):
        arrive(LX.at[d], ls.at[16 + d], lr.at[16 + d])
    LT[1] = jnp.sum(LX[...], axis=0)
    for d in (1, 3, 2):
        send(LT.at[1], LY.at[d], ls.at[20 + d], lr.at[20 + d], step("y", d))
    count = jnp.sum(jnp.where(META[...][:, 0:1, :] >= 0.0, 1.0, 0.0), axis=0)
    count = jnp.sum(count, axis=1, keepdims=True)
    LY[0] = LT[1]
    for d in (1, 3, 2):
        arrive(LY.at[d], ls.at[20 + d], lr.at[20 + d])
    top = jnp.sum(LY[...], axis=0)
    top = jnp.sum(jnp.sum(top, axis=0, keepdims=True), axis=1, keepdims=True) * (1.0 / 2048.0)
    loss[...] = top / count

    for cp in pending:
        cp.wait_send()


def on_device(tokens, expert_ids, gate_values, valid_mask, gate_weight, up_weight, down_weight):
    vmem = pl.BlockSpec(memory_space=pltpu.VMEM)
    hbm = pl.BlockSpec(memory_space=pl.ANY)
    dma = pltpu.SemaphoreType.DMA
    out, loss = pl.pallas_call(
        kernel,
        out_shape=(jax.ShapeDtypeStruct((128, 2048), BF), jax.ShapeDtypeStruct((1, 1), F32)),
        in_specs=[vmem, vmem, vmem, hbm, hbm, hbm, hbm],
        out_specs=(vmem, vmem),
        scratch_shapes=[
            pltpu.VMEM((128, 2048), F32),
            pltpu.VMEM((8, 2, 4, 4, 128, 128), BF),
            pltpu.VMEM((16, 128), F32),
            pltpu.VMEM((16, 16, 128), F32),
            pltpu.VMEM((8, 256, 2048), BF),
            pltpu.VMEM((8, 256, 128), BF),
            pltpu.VMEM((8, 256, 2048), BF),
            pltpu.VMEM((8, 128, 2048), BF),
            pltpu.VMEM((16, 128, 128), BF),
            pltpu.VMEM((16, 128, 128), BF),
            pltpu.VMEM((8, 256, 128), F32),
            pltpu.VMEM((8, 4, 4, 128, 128), BF),
            pltpu.VMEM((8, 4, 4, 128, 128), BF),
            pltpu.VMEM((8, 4, 4, 128, 128), BF),
            pltpu.VMEM((8, 6, 2, 128, 128), BF),
            pltpu.VMEM((8, 3, 128, 128), BF),
            pltpu.VMEM((8, 2, 2, 128, 128), BF),
            pltpu.VMEM((8, 4, 128, 128), BF),
            pltpu.VMEM((8, 128, 128), F32),
            pltpu.VMEM((16, 128, 128), BF),
            pltpu.VMEM((2, 4, 4, 64, 128), BF),
            pltpu.VMEM((8, 128), F32),
            pltpu.VMEM((16, 8, 128), F32),
            pltpu.VMEM((2, 8, 128), F32),
            pltpu.VMEM((4, 8, 128), F32),
            pltpu.VMEM((4, 8, 128), F32),
            dma((4,)), dma((8,)), dma((8,)), dma((16,)), dma((16,)),
            dma((8, 3)), dma((8, 3)), dma((8, 6)), dma((8, 6)),
            dma((8,)), dma((8,)), dma((8,)), dma((8,)),
            dma((8, 6)), dma((8, 6)), dma((8, 3)), dma((8, 3)),
            dma((8,)), dma((8,)), dma((16,)), dma((16,)), dma((24,)), dma((24,)),
        ],
        compiler_params=pltpu.CompilerParams(
            collective_id=0, has_side_effects=True, vmem_limit_bytes=62 * 1024 * 1024),
    )(expert_ids.T, gate_values.T, valid_mask.reshape(1, 128), tokens, gate_weight, up_weight, down_weight)
    return out.astype(F32), loss.reshape(())


def solution(mesh):
    return jax.shard_map(
        on_device,
        mesh=mesh,
        in_specs=(
            P("expert", None),
            P("expert", None),
            P("expert", None),
            P("expert"),
            P("expert", "dp", None),
            P("expert", "dp", None),
            P("expert", "dp", None),
        ),
        out_specs=(P("expert", None), P()),
        check_vma=False,
    )
```

```python
import jax
import jax.numpy as jnp
from jax import lax
from jax.experimental import pallas as pl
from jax.experimental.pallas import tpu as pltpu
from jax.sharding import PartitionSpec as P

MESH = pl.DeviceIdType.MESH
BF = jnp.bfloat16
F32 = jnp.float32
SLOTS = 16
ORDER = (0, 2, 6, 4, 3, 5, 1, 7)
POS = {dz: k for k, dz in enumerate(ORDER)}
GROUPS = ((0,), (2,), (6, 4), (3, 5, 1, 7))
PLANE = (2, 6, 4, 3, 5)
(META_K, SLICE_K, WHOLE_K, A_K, B_K, P_K, Q_K, RB_K, RA_K, V_K, F1_K, F2_K, L_K, LX_K, LY_K) = range(15)
XFIRST = {0: False, 2: True, 6: False, 4: True, 3: False, 5: True, 1: False, 7: True}


def kernel(ids, gates, mask, tok, gw, uw, dw, out, loss,
           TOKF, TOK, MINE, META, X, H, W1, WD, SEL, STR, GS, PART, PX, PEX, RB, RA, ACCB, SUMB, Q, ZR, FIN, LS, LR, LT, LX, LY,
           wsem, out_sem, zr, mr, ar, br, pr, qr, rbr, rar, vr, fr, lr):
    dp = lax.axis_index("dp")
    ex = lax.axis_index("expert")
    y, x = dp // 4, dp % 4
    z, c = ex // 2, ex % 2

    def peer(dz, rc):
        core = c if rc == 0 else 1 - c
        return {"dp": dp, "expert": ((z + dz) % 8) * 2 + core}

    def step(axis, d):
        if axis == "x":
            return {"dp": y * 4 + (x + d + 4) % 4, "expert": ex}
        return {"dp": ((y + d + 4) % 4) * 4 + x, "expert": ex}

    def remote(src, dst, ssem, rsem, dev):
        return pltpu.make_async_remote_copy(
            src_ref=src, dst_ref=dst, send_sem=ssem, recv_sem=rsem, device_id=dev, device_id_type=MESH)

    def send(src, dst, kind, rsem, dev):
        remote(src, dst, out_sem.at[kind], rsem, dev).start()

    def arrive(dst, rsem):
        remote(dst, dst, out_sem.at[0], rsem, peer(0, 1)).wait_recv()

    def sent(kind, like):
        remote(like, like, out_sem.at[kind], mr.at[0], peer(0, 1)).wait_send()

    load = pltpu.make_async_copy(tok, TOKF, wsem.at[3])
    load.start()

    barrier = pltpu.get_barrier_semaphore()
    everyone = [peer(dz, rc) for dz in range(8) for rc in range(2) if (dz, rc) != (0, 0)]
    everyone += [step(axis, d) for axis in "xy" for d in (1, 2, 3)]
    for dev in everyone:
        pl.semaphore_signal(barrier, inc=1, device_id=dev, device_id_type=MESH)

    weights = [
        pltpu.make_async_copy(gw, W1.at[:, pl.ds(0, 96), :], wsem.at[0]),
        pltpu.make_async_copy(uw, W1.at[:, pl.ds(128, 96), :], wsem.at[1]),
        pltpu.make_async_copy(dw, WD.at[:, pl.ds(0, 96), :], wsem.at[2]),
    ]

    valid = jnp.broadcast_to(mask[...], (8, 128)) > 0
    MINE[0:8] = jnp.where(valid, ids[...], -1).astype(F32)
    MINE[8:16] = gates[...]
    META[0] = MINE[...]

    load.wait()
    for w in weights:
        w.start()
    for i in range(4):
        for j in range(4):
            f = (i * 4 + j) * 128
            TOK[0, 0, i, j] = TOKF[:, f:f + 128].astype(BF)
    pl.semaphore_wait(barrier, len(everyone))

    def back(dz):
        return (8 - dz) % 8

    def meta(dz):
        send(MINE, META.at[2 * POS[back(dz)]], META_K, mr.at[2], peer(dz, 0))

    def slice_to(dz):
        send(TOK.at[0, 0, y, x], TOK.at[back(dz), 0, y, x], SLICE_K, zr.at[back(dz)], peer(dz, 0))

    send(MINE, META.at[1], META_K, mr.at[1], peer(0, 1))
    for dz in PLANE[:2]:
        slice_to(back(dz))
    send(TOK.at[0, 0], TOK.at[0, 1], P_K, pr.at[0], peer(0, 1))
    for dz in PLANE[2:]:
        slice_to(back(dz))
    for dz in ORDER[1:]:
        meta(dz)

    def whole():
        send(TOK.at[0, 0], TOK.at[7, 0], WHOLE_K, zr.at[7], peer(1, 0))
        send(TOK.at[0, 0], TOK.at[1, 0], WHOLE_K, zr.at[1], peer(7, 0))

    zero = jnp.zeros((32, 2048), BF)
    for e in range(8):
        W1[e, 96:128, :] = zero
        W1[e, 224:256, :] = zero
        WD[e, 96:128, :] = zero

    def near(dz):
        return ("x", "y", x, y) if XFIRST[dz] else ("y", "x", y, x)

    def wrap(pos):
        return (pos + 8) % 4

    def piece(dz, pos):
        return TOK.at[dz, 0, y, wrap(pos)] if XFIRST[dz] else TOK.at[dz, 0, wrap(pos), x]

    def bundle_half(dz, pos, h):
        two = pl.ds(2 * h, 2)
        return TOK.at[dz, 0, wrap(pos), two] if XFIRST[dz] else TOK.at[dz, 0, two, wrap(pos)]

    def t1(dz):
        a, b, ma, mb = near(dz)
        arrive(TOK.at[dz, 0, y, x], zr.at[dz])
        for d in (2, 1, 3):
            send(piece(dz, ma), piece(dz, ma), A_K, ar.at[PLANE.index(dz)], step(a, d))

    def t3(dz):
        a, b, ma, mb = near(dz)
        k = PLANE.index(dz)
        arrive(RA.at[0], ar.at[k])
        for n, h, d in ((0, 0, 1), (1, 1, -1), (2, 1, 1), (2, 0, -1)):
            send(bundle_half(dz, mb, h), bundle_half(dz, mb, h), B_K, br.at[k, n], step(b, d))

    def t4(dz):
        a, b, ma, mb = near(dz)
        k = PLANE.index(dz)
        for n, h, d in ((0, 0, 1), (1, 1, -1)):
            got = bundle_half(dz, mb - d, h)
            arrive(got, br.at[k, n])
            send(got, got, B_K, br.at[k, 2], step(b, d))

    def t5(dz):
        a, b, ma, mb = near(dz)
        if dz in PLANE:
            arrive(RB.at[dz, pl.ds(2, 4)], br.at[PLANE.index(dz), 2])
        else:
            arrive(TOK.at[dz, 0], zr.at[dz])
        send(TOK.at[dz, 0], TOK.at[dz, 1], P_K, pr.at[dz], peer(0, 1))

    row = lax.broadcasted_iota(jnp.int32, (128, 128), 0)
    col = lax.broadcasted_iota(jnp.int32, (128, 128), 1)
    before = (row < col).astype(F32).astype(BF)
    local = (lax.broadcasted_iota(jnp.int32, (8, 128), 0) + ex * 8).astype(F32)
    slot = lax.broadcasted_iota(jnp.int32, (8, SLOTS, 128), 1).astype(F32)

    def route(k, carry):
        m = META[k]
        named = jnp.zeros((8, 128), F32)
        gate = jnp.zeros((8, 128), F32)
        for i in range(8):
            hit = m[i:i + 1, :] == local
            named = jnp.where(hit, 1.0, named)
            gate = gate + jnp.where(hit, m[8 + i:9 + i, :], 0.0)
        rank = jnp.dot(named.astype(BF), before, preferred_element_type=F32)
        rank = jnp.where(named > 0.0, rank, -1.0)
        pick = jnp.broadcast_to(rank[:, None, :], (8, SLOTS, 128)) == slot
        one = jnp.where(pick, 1.0, 0.0).reshape(128, 128)
        SEL[k] = one.astype(BF)
        STR[k] = one.T.astype(BF)
        held = jnp.where(pick, jnp.broadcast_to(gate[:, None, :], (8, SLOTS, 128)), 0.0)
        GS[:, pl.ds(pl.multiple_of(k * SLOTS, SLOTS), SLOTS), :] = jnp.broadcast_to(
            jnp.sum(held, axis=2, keepdims=True), (8, SLOTS, 128))
        return carry

    def metas1():
        arrive(META.at[pl.ds(0, 7)], mr.at[2])
        for dz in ORDER[1:]:
            k = 2 * POS[dz]
            send(META.at[k], META.at[k + 1], META_K, mr.at[3], peer(0, 1))

    def metas2():
        arrive(META.at[pl.ds(0, 7)], mr.at[3])
        lax.fori_loop(2, 16, route, 0)

    def own_plane():
        arrive(META.at[1], mr.at[1])
        lax.fori_loop(0, 2, route, 0)

    def select(dz, rc):
        if rc:
            arrive(TOK.at[dz, 1], pr.at[dz])
        k = 2 * POS[dz] + rc
        pick = SEL[k]
        for i in range(4):
            rhs = jnp.concatenate([TOK[dz, rc, i, j] for j in range(4)], axis=1)
            got = jnp.dot(pick, rhs, preferred_element_type=F32).astype(BF)
            X[:, k * SLOTS:(k + 1) * SLOTS, i * 512:(i + 1) * 512] = got.reshape(8, SLOTS, 512)

    def span(group):
        lo = 2 * SLOTS * POS[group[0]]
        return lo, lo + 2 * SLOTS * len(group)

    def ups(group, first, last):
        lo, hi = span(group)

        def one(e, carry):
            pre = lax.dot_general(X[e, lo:hi, :], W1[e], (((1,), (1,)), ((), ())), preferred_element_type=F32)
            g, u = pre[:, :128], pre[:, 128:]
            H[e, lo:hi, :] = (g / (1.0 + jnp.exp(-g)) * u).astype(BF)
            return carry

        lax.fori_loop(first, last, one, 0, unroll=2)

    def downs(group, first, last):
        lo, hi = span(group)

        def one(e, carry):
            h = H[e, lo:hi, :]
            scale = GS[e, lo:hi, :]
            scale = jnp.concatenate([scale] * 4, axis=1)
            for i in range(4):
                o = jnp.dot(h, WD[e, :, i * 512:(i + 1) * 512], preferred_element_type=F32)
                X[e, lo:hi, i * 512:(i + 1) * 512] = (o * scale).astype(BF)
            return carry

        lax.fori_loop(first, last, one, 0, unroll=2)

    def combine(dz, rc, i):
        k = 2 * POS[dz] + rc
        rhs = X[:, k * SLOTS:(k + 1) * SLOTS, i * 512:(i + 1) * 512].reshape(128, 512)
        return jnp.dot(STR[k], rhs, preferred_element_type=F32)

    def give(dz):
        for i in range(4):
            got = combine(dz, 1, i).astype(BF)
            for j in range(4):
                PX[dz, i, j] = got[:, j * 128:(j + 1) * 128]
        send(PX.at[dz], PEX.at[dz], Q_K, qr.at[dz], peer(0, 1))

    def home(dz, pos, h):
        two = pl.ds(2 * h, 2)
        return PART.at[dz, wrap(pos), two] if XFIRST[dz] else PART.at[dz, two, wrap(pos)]

    def plus(*refs):
        total = refs[0][...].astype(F32)
        for ref in refs[1:]:
            total = total + ref[...].astype(F32)
        return total

    def r1(dz):
        a, b, ma, mb = near(dz)
        arrive(PEX.at[dz], qr.at[dz])
        for i in range(4):
            got = combine(dz, 0, i)
            for j in range(4):
                PART[dz, i, j] = (got[:, j * 128:(j + 1) * 128] + PEX[dz, i, j].astype(F32)).astype(BF)
        for n, pos, h, d in ((0, 2, 0, 1), (1, 2, 1, -1), (3, -1, 0, -1), (4, 1, 1, 1)):
            send(home(dz, mb + pos, h), RB.at[dz, n], RB_K, rbr.at[dz, min(n, 2)], step(b, d))

    def r2(dz):
        a, b, ma, mb = near(dz)
        for n, d in ((0, 1), (1, -1)):
            arrive(RB.at[dz, n], rbr.at[dz, n])
            ACCB[dz, n] = plus(RB.at[dz, n], home(dz, mb + d, n)).astype(BF)
        for n, d, m in ((0, 1, 2), (1, -1, 5)):
            send(ACCB.at[dz, n], RB.at[dz, m], RB_K, rbr.at[dz, 2], step(b, d))

    def r3(dz):
        a, b, ma, mb = near(dz)
        arrive(RB.at[dz, pl.ds(2, 4)], rbr.at[dz, 2])
        SUMB[dz, 0:2] = plus(home(dz, mb, 0), RB.at[dz, 2], RB.at[dz, 3]).astype(BF)
        SUMB[dz, 2:4] = plus(home(dz, mb, 1), RB.at[dz, 4], RB.at[dz, 5]).astype(BF)
        for d in (2, 1, 3):
            send(SUMB.at[dz, wrap(ma + d)], RA.at[dz, d - 1], RA_K, rar.at[dz], step(a, d))

    def r5(dz):
        a, b, ma, mb = near(dz)
        arrive(RA.at[dz], rar.at[dz])
        Q[dz] = plus(SUMB.at[dz, ma], RA.at[dz, 0], RA.at[dz, 1], RA.at[dz, 2])
        if dz:
            ZR[8 + dz] = Q[dz].astype(BF)
            send(ZR.at[8 + dz], ZR.at[back(dz)], V_K, vr.at[0], peer(dz, 0))

    def each(task, group):
        for dz in group:
            task(dz)

    own_plane()
    select(0, 0)
    select(0, 1)
    for w in weights:
        w.wait()
    ups(GROUPS[0], 0, 4)
    t1(6)
    t1(2)
    ups(GROUPS[0], 4, 8)
    downs(GROUPS[0], 0, 4)
    downs(GROUPS[0], 4, 8)
    t3(6)
    t3(2)
    t1(4)
    give(0)
    t1(3)
    t1(5)
    whole()
    r1(0)
    metas1()
    t4(2)
    t4(6)
    metas2()
    t3(3)
    t3(4)
    t3(5)
    t5(2)
    select(2, 0)
    r2(0)
    t4(4)
    select(2, 1)
    ups(GROUPS[1], 0, 4)
    ups(GROUPS[1], 4, 8)
    t5(6)
    t4(5)
    downs(GROUPS[1], 0, 4)
    t4(3)
    downs(GROUPS[1], 4, 8)
    give(2)
    select(6, 0)
    select(6, 1)
    t5(4)
    select(4, 0)
    t5(1)
    select(1, 0)
    r3(0)
    r1(2)
    t5(5)
    select(5, 0)
    t5(7)
    select(7, 0)
    select(4, 1)
    t5(3)
    select(3, 0)
    ups(GROUPS[2], 0, 4)
    r5(0)
    ups(GROUPS[2], 4, 8)
    downs(GROUPS[2], 0, 4)
    select(5, 1)
    downs(GROUPS[2], 4, 8)
    give(6)
    select(3, 1)
    give(4)
    select(1, 1)
    r2(2)
    select(7, 1)
    ups(GROUPS[3], 0, 4)
    r1(6)
    r1(4)
    ups(GROUPS[3], 4, 8)
    downs(GROUPS[3], 0, 4)
    r2(6)
    downs(GROUPS[3], 4, 8)
    give(3)
    give(5)
    r2(4)
    give(7)
    r3(2)
    give(1)
    r3(6)
    r1(3)
    r1(5)
    r5(2)
    r3(4)
    r1(7)
    r5(6)
    r2(3)
    r1(1)
    r2(5)
    r5(4)
    r3(3)
    r2(7)
    r2(1)
    r3(5)
    r5(3)
    r3(1)
    r3(7)
    r5(5)
    r5(1)
    r5(7)
    arrive(ZR.at[pl.ds(1, 7)], vr.at[0])
    total = Q[0]
    for dz in ORDER[1:]:
        total = total + ZR[dz].astype(F32)
    FIN[0, y, x] = total[0:64].astype(BF)
    FIN[1, y, x] = total[64:128].astype(BF)
    LS[...] = jnp.sum((total * total).reshape(16, 8, 128), axis=0)

    def strip(h, first, pos):
        if first:
            return FIN.at[0, y, wrap(pos)] if h == 0 else FIN.at[1, wrap(pos), x]
        return FIN.at[0, wrap(pos)] if h == 0 else FIN.at[1, :, wrap(pos)]

    def gather(first):
        legs = (("x", x), ("y", y)) if first else (("y", y), ("x", x))
        for d in (2, 1, 3):
            for h, (axis, me) in enumerate(legs):
                send(strip(h, first, me), strip(h, first, me), F1_K if first else F2_K,
                     fr.at[0 if first else 1], step(axis, d))

    gather(True)
    for dz in (4, 3, 5, 2, 6, 1, 7, 0):
        for rc in range(2):
            if (dz, rc) != (0, 0):
                send(LS, LR.at[2 * POS[back(dz)] + rc], L_K, lr.at[0], peer(dz, rc))
    LR[0] = LS[...]
    count = jnp.sum(jnp.where(META[...][:, 0:1, :] >= 0.0, 1.0, 0.0), axis=0)
    count = jnp.sum(count, axis=1, keepdims=True)
    arrive(RA.at[0], fr.at[0])
    gather(False)

    arrive(LR.at[pl.ds(1, 15)], lr.at[0])
    LT[0] = jnp.sum(LR[...], axis=0)
    LX[0] = LT[0]
    for d in (2, 1, 3):
        send(LT.at[0], LX.at[d], LX_K, lr.at[1], step("x", d))
    arrive(LX.at[pl.ds(1, 3)], lr.at[1])
    LT[1] = jnp.sum(LX[...], axis=0)
    LY[0] = LT[1]
    for d in (2, 1, 3):
        send(LT.at[1], LY.at[d], LY_K, lr.at[2], step("y", d))
    arrive(RB.at[0], fr.at[1])
    for i in range(4):
        for j in range(4):
            f = (i * 4 + j) * 128
            out[0:64, f:f + 128] = FIN[0, i, j].astype(out.dtype)
            out[64:128, f:f + 128] = FIN[1, i, j].astype(out.dtype)
    arrive(LY.at[pl.ds(1, 3)], lr.at[2])
    top = jnp.sum(LY[...], axis=0)
    top = jnp.sum(jnp.sum(top, axis=0, keepdims=True), axis=1, keepdims=True) * (1.0 / 2048.0)
    loss[...] = top / count

    for kind, like in (
        (META_K, META.at[pl.ds(1, 15)]), (SLICE_K, ZR.at[pl.ds(0, 5)]), (WHOLE_K, PX.at[pl.ds(0, 2)]),
        (A_K, RA.at[pl.ds(0, 5)]), (B_K, RB.at[pl.ds(0, 5)]), (P_K, PX), (Q_K, PX), (RB_K, RB), (RA_K, RA),
        (V_K, ZR.at[pl.ds(1, 7)]), (F1_K, RA.at[0]), (F2_K, RB.at[0]), (L_K, LR.at[pl.ds(1, 15)]),
        (LX_K, LX.at[pl.ds(1, 3)]), (LY_K, LY.at[pl.ds(1, 3)]),
    ):
        sent(kind, like)


def on_device(tokens, expert_ids, gate_values, valid_mask, gate_weight, up_weight, down_weight):
    vmem = pl.BlockSpec(memory_space=pltpu.VMEM)
    hbm = pl.BlockSpec(memory_space=pl.ANY)
    dma = pltpu.SemaphoreType.DMA
    out, loss = pl.pallas_call(
        kernel,
        out_shape=(jax.ShapeDtypeStruct((128, 2048), BF), jax.ShapeDtypeStruct((1, 1), F32)),
        in_specs=[vmem, vmem, vmem, hbm, hbm, hbm, hbm],
        out_specs=(vmem, vmem),
        scratch_shapes=[
            pltpu.VMEM((128, 2048), F32),
            pltpu.VMEM((8, 2, 4, 4, 128, 128), BF),
            pltpu.VMEM((16, 128), F32),
            pltpu.VMEM((16, 16, 128), F32),
            pltpu.VMEM((8, 256, 2048), BF),
            pltpu.VMEM((8, 256, 128), BF),
            pltpu.VMEM((8, 256, 2048), BF),
            pltpu.VMEM((8, 128, 2048), BF),
            pltpu.VMEM((16, 128, 128), BF),
            pltpu.VMEM((16, 128, 128), BF),
            pltpu.VMEM((8, 256, 128), F32),
            pltpu.VMEM((8, 4, 4, 128, 128), BF),
            pltpu.VMEM((8, 4, 4, 128, 128), BF),
            pltpu.VMEM((8, 4, 4, 128, 128), BF),
            pltpu.VMEM((8, 6, 2, 128, 128), BF),
            pltpu.VMEM((8, 3, 128, 128), BF),
            pltpu.VMEM((8, 2, 2, 128, 128), BF),
            pltpu.VMEM((8, 4, 128, 128), BF),
            pltpu.VMEM((8, 128, 128), F32),
            pltpu.VMEM((16, 128, 128), BF),
            pltpu.VMEM((2, 4, 4, 64, 128), BF),
            pltpu.VMEM((8, 128), F32),
            pltpu.VMEM((16, 8, 128), F32),
            pltpu.VMEM((2, 8, 128), F32),
            pltpu.VMEM((4, 8, 128), F32),
            pltpu.VMEM((4, 8, 128), F32),
            dma((4,)), dma((15,)), dma((8,)), dma((4,)), dma((5,)), dma((5, 3)), dma((8,)), dma((8,)),
            dma((8, 3)), dma((8,)), dma((1,)), dma((2,)), dma((3,)),
        ],
        compiler_params=pltpu.CompilerParams(
            collective_id=0, has_side_effects=True, vmem_limit_bytes=62 * 1024 * 1024),
    )(expert_ids.T, gate_values.T, valid_mask.reshape(1, 128), tokens, gate_weight, up_weight, down_weight)
    return out.astype(F32), loss.reshape(())


def solution(mesh):
    return jax.shard_map(
        on_device,
        mesh=mesh,
        in_specs=(
            P("expert", None),
            P("expert", None),
            P("expert", None),
            P("expert"),
            P("expert", "dp", None),
            P("expert", "dp", None),
            P("expert", "dp", None),
        ),
        out_specs=(P("expert", None), P()),
        check_vma=False,
    )
```

```python
import jax
import jax.numpy as jnp
from jax import lax
from jax.experimental import pallas as pl
from jax.experimental.pallas import tpu as pltpu
from jax.sharding import PartitionSpec as P

MESH = pl.DeviceIdType.MESH
BF = jnp.bfloat16
F32 = jnp.float32
SLOTS = 16
ORDER = (0, 2, 6, 3, 5, 4, 1, 7)
POS = {dz: k for k, dz in enumerate(ORDER)}
GROUPS = ((0,), (2, 6, 3), (5, 4, 1, 7))
PLANE = (2, 6, 3, 5, 4)
FAST_OUT, FAST_IN = (6,), ()
(META_K, SLICE_K, WHOLE_K, A_K, B_K, P_K, Q_K, RB_K, RA_K, V_K, F1_K, F2_K, L_K, LX_K) = range(14)
XFIRST = {0: False, 2: True, 6: False, 3: True, 5: False, 4: True, 1: False, 7: True}


def kernel(ids, gates, mask, tok, gw, uw, dw, out, loss,
           TOKF, TOK, MINE, META, X, H, W1, WD, SEL, STR, GS, PART, PX, PEX, RB, RA, ACCB, SUMB, Q, ZR, FIN, LS, LR, LT, LX,
           wsem, out_sem, zr, mr, ar, br, pr, qr, rbr, rar, vr, fr, lr):
    dp = lax.axis_index("dp")
    ex = lax.axis_index("expert")
    y, x = dp // 4, dp % 4
    z, c = ex // 2, ex % 2

    def peer(dz, rc):
        core = c if rc == 0 else 1 - c
        return {"dp": dp, "expert": ((z + dz) % 8) * 2 + core}

    def step(axis, d):
        if axis == "x":
            return {"dp": y * 4 + (x + d + 4) % 4, "expert": ex}
        return {"dp": ((y + d + 4) % 4) * 4 + x, "expert": ex}

    def across(i, j):
        return {"dp": ((y + i) % 4) * 4 + (x + j) % 4, "expert": ex}

    def remote(src, dst, ssem, rsem, dev):
        return pltpu.make_async_remote_copy(
            src_ref=src, dst_ref=dst, send_sem=ssem, recv_sem=rsem, device_id=dev, device_id_type=MESH)

    def send(src, dst, kind, rsem, dev):
        remote(src, dst, out_sem.at[kind], rsem, dev).start()

    def arrive(dst, rsem):
        remote(dst, dst, out_sem.at[0], rsem, peer(0, 1)).wait_recv()

    def sent(kind, like):
        remote(like, like, out_sem.at[kind], mr.at[0], peer(0, 1)).wait_send()

    load = pltpu.make_async_copy(tok, TOKF, wsem.at[3])
    load.start()

    barrier = pltpu.get_barrier_semaphore()
    everyone = [peer(dz, rc) for dz in range(8) for rc in range(2) if (dz, rc) != (0, 0)]
    everyone += [across(i, j) for i in range(4) for j in range(4) if (i, j) != (0, 0)]
    for dev in everyone:
        pl.semaphore_signal(barrier, inc=1, device_id=dev, device_id_type=MESH)

    weights = [
        pltpu.make_async_copy(gw, W1.at[:, pl.ds(0, 96), :], wsem.at[0]),
        pltpu.make_async_copy(uw, W1.at[:, pl.ds(128, 96), :], wsem.at[1]),
        pltpu.make_async_copy(dw, WD.at[:, pl.ds(0, 96), :], wsem.at[2]),
    ]

    valid = jnp.broadcast_to(mask[...], (8, 128)) > 0
    MINE[0:8] = jnp.where(valid, ids[...], -1).astype(F32)
    MINE[8:16] = gates[...]
    META[0] = MINE[...]

    load.wait()
    for w in weights:
        w.start()
    for i in range(4):
        for j in range(4):
            f = (i * 4 + j) * 128
            TOK[0, 0, i, j] = TOKF[:, f:f + 128].astype(BF)
    pl.semaphore_wait(barrier, len(everyone))

    def back(dz):
        return (8 - dz) % 8

    def meta(dz):
        send(MINE, META.at[2 * POS[back(dz)]], META_K, mr.at[2], peer(dz, 0))

    def slice_to(dz):
        send(TOK.at[0, 0, y, x], TOK.at[back(dz), 0, y, x], SLICE_K, zr.at[back(dz)], peer(dz, 0))

    send(MINE, META.at[1], META_K, mr.at[1], peer(0, 1))
    for dz in PLANE[:2]:
        slice_to(back(dz))
    send(TOK.at[0, 0], TOK.at[0, 1], P_K, pr.at[0], peer(0, 1))
    for dz in PLANE[2:]:
        slice_to(back(dz))
    for dz in ORDER[1:]:
        meta(dz)

    def whole():
        send(TOK.at[0, 0], TOK.at[7, 0], WHOLE_K, zr.at[7], peer(1, 0))
        send(TOK.at[0, 0], TOK.at[1, 0], WHOLE_K, zr.at[1], peer(7, 0))

    zero = jnp.zeros((32, 2048), BF)
    for e in range(8):
        W1[e, 96:128, :] = zero
        W1[e, 224:256, :] = zero
        WD[e, 96:128, :] = zero

    def near(dz):
        return ("x", "y", x, y) if XFIRST[dz] else ("y", "x", y, x)

    def wrap(pos):
        return (pos + 8) % 4

    def piece(dz, pos):
        return TOK.at[dz, 0, y, wrap(pos)] if XFIRST[dz] else TOK.at[dz, 0, wrap(pos), x]

    def bundle_half(dz, pos, h):
        two = pl.ds(2 * h, 2)
        return TOK.at[dz, 0, wrap(pos), two] if XFIRST[dz] else TOK.at[dz, 0, two, wrap(pos)]

    def t1(dz):
        a, b, ma, mb = near(dz)
        arrive(TOK.at[dz, 0, y, x], zr.at[dz])
        for d in (2, 1, 3):
            send(piece(dz, ma), piece(dz, ma), A_K, ar.at[PLANE.index(dz)], step(a, d))

    def t3(dz):
        a, b, ma, mb = near(dz)
        k = PLANE.index(dz)
        arrive(RA.at[0], ar.at[k])
        if dz in FAST_OUT:
            for d in (2, 1, 3):
                for h in range(2):
                    send(bundle_half(dz, mb, h), bundle_half(dz, mb, h), B_K, br.at[k, 2], step(b, d))
            return
        for n, h, d in ((0, 0, 1), (1, 1, -1), (2, 1, 1), (2, 0, -1)):
            send(bundle_half(dz, mb, h), bundle_half(dz, mb, h), B_K, br.at[k, n], step(b, d))

    def t4(dz):
        a, b, ma, mb = near(dz)
        k = PLANE.index(dz)
        if dz in FAST_OUT:
            return
        for n, h, d in ((0, 0, 1), (1, 1, -1)):
            got = bundle_half(dz, mb - d, h)
            arrive(got, br.at[k, n])
            send(got, got, B_K, br.at[k, 2], step(b, d))

    def t5(dz):
        a, b, ma, mb = near(dz)
        if dz in PLANE:
            arrive(RB.at[dz] if dz in FAST_OUT else RB.at[dz, pl.ds(2, 4)], br.at[PLANE.index(dz), 2])
        else:
            arrive(TOK.at[dz, 0], zr.at[dz])
        send(TOK.at[dz, 0], TOK.at[dz, 1], P_K, pr.at[dz], peer(0, 1))

    row = lax.broadcasted_iota(jnp.int32, (128, 128), 0)
    col = lax.broadcasted_iota(jnp.int32, (128, 128), 1)
    before = (row < col).astype(F32).astype(BF)
    local = (lax.broadcasted_iota(jnp.int32, (8, 128), 0) + ex * 8).astype(F32)
    slot = lax.broadcasted_iota(jnp.int32, (8, SLOTS, 128), 1).astype(F32)

    def route(k, carry):
        m = META[k]
        named = jnp.zeros((8, 128), F32)
        gate = jnp.zeros((8, 128), F32)
        for i in range(8):
            hit = m[i:i + 1, :] == local
            named = jnp.where(hit, 1.0, named)
            gate = gate + jnp.where(hit, m[8 + i:9 + i, :], 0.0)
        rank = jnp.dot(named.astype(BF), before, preferred_element_type=F32)
        rank = jnp.where(named > 0.0, rank, -1.0)
        pick = jnp.broadcast_to(rank[:, None, :], (8, SLOTS, 128)) == slot
        one = jnp.where(pick, 1.0, 0.0).reshape(128, 128)
        SEL[k] = one.astype(BF)
        STR[k] = one.T.astype(BF)
        held = jnp.where(pick, jnp.broadcast_to(gate[:, None, :], (8, SLOTS, 128)), 0.0)
        GS[:, pl.ds(pl.multiple_of(k * SLOTS, SLOTS), SLOTS), :] = jnp.broadcast_to(
            jnp.sum(held, axis=2, keepdims=True), (8, SLOTS, 128))
        return carry

    def metas1():
        arrive(META.at[pl.ds(0, 7)], mr.at[2])
        for dz in ORDER[1:]:
            k = 2 * POS[dz]
            send(META.at[k], META.at[k + 1], META_K, mr.at[3], peer(0, 1))

    def metas2():
        arrive(META.at[pl.ds(0, 7)], mr.at[3])
        lax.fori_loop(2, 16, route, 0)

    def own_plane():
        arrive(META.at[1], mr.at[1])
        lax.fori_loop(0, 2, route, 0)

    def select(dz, rc):
        if rc:
            arrive(TOK.at[dz, 1], pr.at[dz])
        k = 2 * POS[dz] + rc
        pick = SEL[k]
        for i in range(4):
            rhs = jnp.concatenate([TOK[dz, rc, i, j] for j in range(4)], axis=1)
            got = jnp.dot(pick, rhs, preferred_element_type=F32).astype(BF)
            X[:, k * SLOTS:(k + 1) * SLOTS, i * 512:(i + 1) * 512] = got.reshape(8, SLOTS, 512)

    def span(group):
        lo = 2 * SLOTS * POS[group[0]]
        return lo, lo + 2 * SLOTS * len(group)

    def ups(group, first, last):
        lo, hi = span(group)

        def one(e, carry):
            pre = lax.dot_general(X[e, lo:hi, :], W1[e], (((1,), (1,)), ((), ())), preferred_element_type=F32)
            g, u = pre[:, :128], pre[:, 128:]
            H[e, lo:hi, :] = (g / (1.0 + jnp.exp(-g)) * u).astype(BF)
            return carry

        lax.fori_loop(first, last, one, 0, unroll=2)

    def downs(group, first, last):
        lo, hi = span(group)

        def one(e, carry):
            h = H[e, lo:hi, :]
            scale = GS[e, lo:hi, :]
            scale = jnp.concatenate([scale] * 4, axis=1)
            for i in range(4):
                o = jnp.dot(h, WD[e, :, i * 512:(i + 1) * 512], preferred_element_type=F32)
                X[e, lo:hi, i * 512:(i + 1) * 512] = (o * scale).astype(BF)
            return carry

        lax.fori_loop(first, last, one, 0, unroll=2)

    def combine(dz, rc, i):
        k = 2 * POS[dz] + rc
        rhs = X[:, k * SLOTS:(k + 1) * SLOTS, i * 512:(i + 1) * 512].reshape(128, 512)
        return jnp.dot(STR[k], rhs, preferred_element_type=F32)

    def give(dz):
        for i in range(4):
            got = combine(dz, 1, i).astype(BF)
            for j in range(4):
                PX[dz, i, j] = got[:, j * 128:(j + 1) * 128]
        send(PX.at[dz], PEX.at[dz], Q_K, qr.at[dz], peer(0, 1))

    def home(dz, pos, h):
        two = pl.ds(2 * h, 2)
        return PART.at[dz, wrap(pos), two] if XFIRST[dz] else PART.at[dz, two, wrap(pos)]

    def plus(*refs):
        total = refs[0][...].astype(F32)
        for ref in refs[1:]:
            total = total + ref[...].astype(F32)
        return total

    def r1(dz):
        a, b, ma, mb = near(dz)
        arrive(PEX.at[dz], qr.at[dz])
        for i in range(4):
            got = combine(dz, 0, i)
            for j in range(4):
                PART[dz, i, j] = (got[:, j * 128:(j + 1) * 128] + PEX[dz, i, j].astype(F32)).astype(BF)
        if dz in FAST_IN:
            for d in (2, 1, 3):
                for h in range(2):
                    send(home(dz, mb + d, h), RB.at[dz, 2 * d - 2 + h], RB_K, rbr.at[dz, 2], step(b, d))
            return
        for n, pos, h, d in ((0, 2, 0, 1), (1, 2, 1, -1), (3, -1, 0, -1), (4, 1, 1, 1)):
            send(home(dz, mb + pos, h), RB.at[dz, n], RB_K, rbr.at[dz, min(n, 2)], step(b, d))

    def r2(dz):
        a, b, ma, mb = near(dz)
        if dz in FAST_IN:
            return
        for n, d in ((0, 1), (1, -1)):
            arrive(RB.at[dz, n], rbr.at[dz, n])
            ACCB[dz, n] = plus(RB.at[dz, n], home(dz, mb + d, n)).astype(BF)
        for n, d, m in ((0, 1, 2), (1, -1, 5)):
            send(ACCB.at[dz, n], RB.at[dz, m], RB_K, rbr.at[dz, 2], step(b, d))

    def r3(dz):
        a, b, ma, mb = near(dz)
        arrive(RB.at[dz] if dz in FAST_IN else RB.at[dz, pl.ds(2, 4)], rbr.at[dz, 2])
        low, high = ((0, 2, 4), (1, 3, 5)) if dz in FAST_IN else ((2, 3), (4, 5))
        SUMB[dz, 0:2] = plus(home(dz, mb, 0), *[RB.at[dz, n] for n in low]).astype(BF)
        SUMB[dz, 2:4] = plus(home(dz, mb, 1), *[RB.at[dz, n] for n in high]).astype(BF)
        for d in (2, 1, 3):
            send(SUMB.at[dz, wrap(ma + d)], RA.at[dz, d - 1], RA_K, rar.at[dz], step(a, d))

    def r5(dz):
        a, b, ma, mb = near(dz)
        arrive(RA.at[dz], rar.at[dz])
        Q[dz] = plus(SUMB.at[dz, ma], RA.at[dz, 0], RA.at[dz, 1], RA.at[dz, 2])
        if dz:
            ZR[8 + dz] = Q[dz].astype(BF)
            send(ZR.at[8 + dz], ZR.at[back(dz)], V_K, vr.at[0], peer(dz, 0))

    def each(task, group):
        for dz in group:
            task(dz)

    own_plane()
    select(0, 0)
    select(0, 1)
    for w in weights:
        w.wait()
    ups(GROUPS[0], 0, 4)
    ups(GROUPS[0], 4, 8)
    t1(2)
    t1(6)
    downs(GROUPS[0], 0, 4)
    downs(GROUPS[0], 4, 8)
    give(0)
    t1(3)
    t1(5)
    t3(2)
    t3(6)
    t4(6)
    r1(0)
    t1(4)
    whole()
    t3(3)
    t3(5)
    metas1()
    metas2()
    t4(2)
    t5(6)
    select(6, 0)
    t4(3)
    r2(0)
    select(6, 1)
    t5(2)
    select(2, 0)
    t3(4)
    t5(3)
    select(3, 0)
    select(2, 1)
    t4(5)
    select(3, 1)
    ups(GROUPS[1], 0, 4)
    t5(1)
    t5(7)
    t4(4)
    ups(GROUPS[1], 4, 8)
    t5(5)
    downs(GROUPS[1], 0, 4)
    downs(GROUPS[1], 4, 8)
    give(2)
    select(7, 1)
    t5(4)
    select(4, 0)
    select(5, 0)
    give(3)
    select(5, 1)
    select(1, 1)
    r3(0)
    give(6)
    select(7, 0)
    r1(2)
    select(1, 0)
    select(4, 1)
    ups(GROUPS[2], 0, 4)
    r1(3)
    r1(6)
    ups(GROUPS[2], 4, 8)
    r2(2)
    downs(GROUPS[2], 0, 4)
    downs(GROUPS[2], 4, 8)
    r2(6)
    give(5)
    give(4)
    give(7)
    give(1)
    r2(3)
    r5(0)
    r3(2)
    r1(5)
    r3(6)
    r1(4)
    r1(7)
    r3(3)
    r5(2)
    r1(1)
    r2(5)
    r5(6)
    r2(4)
    r5(3)
    r2(1)
    r2(7)
    r3(5)
    r3(4)
    r3(1)
    r3(7)
    r5(5)
    r5(4)
    r5(1)
    r5(7)
    arrive(ZR.at[pl.ds(1, 7)], vr.at[0])
    total = Q[0]
    for dz in ORDER[1:]:
        total = total + ZR[dz].astype(F32)
    FIN[0, y, x] = total[0:64].astype(BF)
    FIN[1, y, x] = total[64:128].astype(BF)
    LS[...] = jnp.sum((total * total).reshape(16, 8, 128), axis=0)

    def strip(h, first, pos):
        if first:
            return FIN.at[0, y, wrap(pos)] if h == 0 else FIN.at[1, wrap(pos), x]
        return FIN.at[0, wrap(pos)] if h == 0 else FIN.at[1, :, wrap(pos)]

    def gather(first):
        legs = (("x", x), ("y", y)) if first else (("y", y), ("x", x))
        for d in (2, 1, 3):
            for h, (axis, me) in enumerate(legs):
                send(strip(h, first, me), strip(h, first, me), F1_K if first else F2_K,
                     fr.at[0 if first else 1], step(axis, d))

    gather(True)
    for dz in (4, 3, 5, 2, 6, 1, 7, 0):
        for rc in range(2):
            if (dz, rc) != (0, 0):
                send(LS, LR.at[ex], L_K, lr.at[0], peer(dz, rc))
    LR[ex] = LS[...]
    count = jnp.sum(jnp.where(META[...][:, 0:1, :] >= 0.0, 1.0, 0.0), axis=0)
    count = jnp.sum(count, axis=1, keepdims=True)
    arrive(RA.at[0], fr.at[0])
    gather(False)

    arrive(LR.at[pl.ds(1, 15)], lr.at[0])
    LT[0] = jnp.sum(LR[...], axis=0)
    LX[dp] = LT[0]
    for i in range(4):
        for j in range(4):
            if (i, j) != (0, 0):
                send(LT.at[0], LX.at[dp], LX_K, lr.at[1], across(i, j))
    arrive(RB.at[0], fr.at[1])
    for i in range(4):
        for j in range(4):
            f = (i * 4 + j) * 128
            out[0:64, f:f + 128] = FIN[0, i, j].astype(out.dtype)
            out[64:128, f:f + 128] = FIN[1, i, j].astype(out.dtype)
    arrive(LX.at[pl.ds(1, 15)], lr.at[1])
    top = jnp.sum(LX[...], axis=0)
    top = jnp.sum(jnp.sum(top, axis=0, keepdims=True), axis=1, keepdims=True) * (1.0 / 2048.0)
    loss[...] = top / count

    for kind, like in (
        (META_K, META.at[pl.ds(1, 15)]), (SLICE_K, ZR.at[pl.ds(0, 5)]), (WHOLE_K, PX.at[pl.ds(0, 2)]),
        (A_K, RA.at[pl.ds(0, 5)]), (B_K, RB.at[pl.ds(0, 5)]), (P_K, PX), (Q_K, PX), (RB_K, RB), (RA_K, RA),
        (V_K, ZR.at[pl.ds(1, 7)]), (F1_K, RA.at[0]), (F2_K, RB.at[0]), (L_K, LR.at[pl.ds(1, 15)]),
        (LX_K, LX.at[pl.ds(1, 15)]),
    ):
        sent(kind, like)


def on_device(tokens, expert_ids, gate_values, valid_mask, gate_weight, up_weight, down_weight):
    vmem = pl.BlockSpec(memory_space=pltpu.VMEM)
    hbm = pl.BlockSpec(memory_space=pl.ANY)
    dma = pltpu.SemaphoreType.DMA
    out, loss = pl.pallas_call(
        kernel,
        out_shape=(jax.ShapeDtypeStruct((128, 2048), BF), jax.ShapeDtypeStruct((1, 1), F32)),
        in_specs=[vmem, vmem, vmem, hbm, hbm, hbm, hbm],
        out_specs=(vmem, vmem),
        scratch_shapes=[
            pltpu.VMEM((128, 2048), F32),
            pltpu.VMEM((8, 2, 4, 4, 128, 128), BF),
            pltpu.VMEM((16, 128), F32),
            pltpu.VMEM((16, 16, 128), F32),
            pltpu.VMEM((8, 256, 2048), BF),
            pltpu.VMEM((8, 256, 128), BF),
            pltpu.VMEM((8, 256, 2048), BF),
            pltpu.VMEM((8, 128, 2048), BF),
            pltpu.VMEM((16, 128, 128), BF),
            pltpu.VMEM((16, 128, 128), BF),
            pltpu.VMEM((8, 256, 128), F32),
            pltpu.VMEM((8, 4, 4, 128, 128), BF),
            pltpu.VMEM((8, 4, 4, 128, 128), BF),
            pltpu.VMEM((8, 4, 4, 128, 128), BF),
            pltpu.VMEM((8, 6, 2, 128, 128), BF),
            pltpu.VMEM((8, 3, 128, 128), BF),
            pltpu.VMEM((8, 2, 2, 128, 128), BF),
            pltpu.VMEM((8, 4, 128, 128), BF),
            pltpu.VMEM((8, 128, 128), F32),
            pltpu.VMEM((16, 128, 128), BF),
            pltpu.VMEM((2, 4, 4, 64, 128), BF),
            pltpu.VMEM((8, 128), F32),
            pltpu.VMEM((16, 8, 128), F32),
            pltpu.VMEM((1, 8, 128), F32),
            pltpu.VMEM((16, 8, 128), F32),
            dma((4,)), dma((14,)), dma((8,)), dma((4,)), dma((5,)), dma((5, 3)), dma((8,)), dma((8,)),
            dma((8, 3)), dma((8,)), dma((1,)), dma((2,)), dma((2,)),
        ],
        compiler_params=pltpu.CompilerParams(
            collective_id=0, has_side_effects=True, vmem_limit_bytes=62 * 1024 * 1024),
    )(expert_ids.T, gate_values.T, valid_mask.reshape(1, 128), tokens, gate_weight, up_weight, down_weight)
    return out.astype(F32), loss.reshape(())


def solution(mesh):
    return jax.shard_map(
        on_device,
        mesh=mesh,
        in_specs=(
            P("expert", None),
            P("expert", None),
            P("expert", None),
            P("expert"),
            P("expert", "dp", None),
            P("expert", "dp", None),
            P("expert", "dp", None),
        ),
        out_specs=(P("expert", None), P()),
        check_vma=False,
    )
```
